32 devices in a mesh: dp: 8 (over y, x, core), ctx: 4 (over z).
Axes of the slice: x: 2, y: 2, z: 4, core: 2. Of those that a mesh axis runs over, the one named last changes fastest.
Arguments:
- normed: bfloat16 [8, 512, 5376], P('dp', 'ctx'), may hold values from -6 to 6
- queries: bfloat16 [8, 512, 2048], P('dp', 'ctx'), may hold values from -8 to 8
- keys: bfloat16 [8, 512, 1024], P('dp', 'ctx'), may hold values from -8 to 8
- values: bfloat16 [8, 512, 1024], P('dp', 'ctx'), may hold values from -6 to 6
- out_grad: bfloat16 [8, 512, 2048], P('dp', 'ctx'), may hold values from -150 to 150
- segment_ids: int32 [8, 512], P('dp'), may hold values from 0 to 3, never falling along the last dimension, each value on 1 to 384 neighbouring positions
Outputs:
- grad_queries: bfloat16 [8, 512, 2048], P('dp', 'ctx')
- grad_keys: bfloat16 [8, 512, 1024], P('dp', 'ctx')
- grad_values: bfloat16 [8, 512, 1024], P('dp', 'ctx')
- grad_weight: bfloat16 [5376, 1024], P('ctx', 'dp')
The draws below stay inside these ranges and needn't reach their ends.
Inputs may be any that keep to these rules, and one draw needn't show every extreme that they name: `segment_ids`: within a sequence the document numbers never fall, and a document has at most 384 positions.
All inputs are finite; a program needn't handle non-finite values.
Results may differ from the reference program's by a relative error of at most 0.022.
Values may be sent and summed in bfloat16 or wider, within the bound.
A program may use at most 128 MiB of HBM per device.

```python
import math
import jax
import jax.numpy as jnp
import numpy as np
from jax import lax

D = 5376
QUERY_HEADS = 16
KEY_VALUE_HEADS = 8
HEAD_SIZE = 128
WINDOW = 1024
DOCS = 4
TOK_DEV = 128
SEQUENCE_COUNT = 8
SEQUENCE_LENGTH = 512
ALL_TOK = 4096
N_CTX = 4


def draw_queries(key, part):
    sampled_values = jax.random.normal(jax.random.fold_in(key, 11), (SEQUENCE_COUNT, SEQUENCE_LENGTH, QUERY_HEADS * HEAD_SIZE), jnp.float32)
    return jnp.clip(sampled_values, -8.0, 8.0).astype(jnp.bfloat16)


def draw_keys(key, part):
    sampled_values = jax.random.normal(jax.random.fold_in(key, 13), (SEQUENCE_COUNT, SEQUENCE_LENGTH, KEY_VALUE_HEADS * HEAD_SIZE), jnp.float32)
    return jnp.clip(sampled_values, -8.0, 8.0).astype(jnp.bfloat16)


def with_spikes(array, key, source, target, parts, factor):
    owner, partner = [(jnp.arange(array.shape[position]) // (array.shape[position] // parts)).reshape([-1 if axis == position else 1 for axis in range(array.ndim)]) for position in (source, target)]
    chosen = jax.random.permutation(key, parts)[partner]
    strong = (owner == chosen) | (owner == (partner + parts // 2) % parts)
    return jnp.where(strong, factor * array, array)


def steps_of(rng, extent, cuts, low, top_value):
    def one(axis_at, blocks):
        steps = jax.random.uniform(jax.random.fold_in(jax.random.fold_in(rng, 6), axis_at), (blocks,), jnp.float32, low / len(cuts), top_value / len(cuts))
        return jnp.repeat(jnp.exp(steps), extent[axis_at] // blocks).reshape((-1,) + (1,) * (len(extent) - axis_at - 1))

    loudness = one(*cuts[0])
    for cut in cuts[1:]:
        loudness = loudness * one(*cut)
    return loudness


def profile(number_of, total, limit, slope):
    loads = [(1 << 20) // math.isqrt(standing ** slope) + 1 for standing in range(2, number_of + 1)]
    surplus, given = total - limit - (number_of - 1), [1] * (number_of - 1)
    while surplus > 0:
        candidates = [i for i in range(number_of - 1) if given[i] < limit]
        mass, left = sum([loads[i] for i in candidates]), surplus
        for i in candidates:
            addition = min(limit - given[i], max(1, left * loads[i] // mass), surplus)
            given[i] = given[i] + addition
            surplus = surplus - addition
    return np.array([limit] + given)


def uneven_parts(own_key, count, total, reach, lean):
    if count == 2:
        one = jax.random.randint(own_key, (), max(1, total - reach), min(reach, total - 1) + 1)
        return jnp.stack([one, total - one])
    tallies = jnp.asarray(profile(count, total, reach, lean), jnp.int32)
    twos = (count - 1) // 2
    donor, taker = tallies[1:1 + 2 * twos:2], tallies[2:2 + 2 * twos:2]
    room = jnp.minimum(donor - 1, reach - taker)
    shifted = jax.random.randint(jax.random.fold_in(own_key, 1), (twos,), 0, 1 << 20) % (room + 1)
    tallies = tallies.at[1:1 + 2 * twos:2].set(donor - shifted).at[2:2 + 2 * twos:2].set(taker + shifted)
    return tallies[jax.random.permutation(jax.random.fold_in(own_key, 2), count)]


def gaussian(stream_key, dims, spread, limit, cuts=(), held_as=jnp.bfloat16):
    values = jax.random.normal(stream_key, dims, jnp.float32) * spread
    if len(cuts) > 0:
        values = steps_of(stream_key, dims, cuts, -0.22, 0.18) * values
    return jnp.clip(values, min=-limit, max=limit).astype(held_as)


def noise_with(key, extent, scale, reach, shards, heavy, held_as=jnp.bfloat16):
    entries = scale * jax.random.normal(key, extent, jnp.float32)
    if shards:
        entries = entries * steps_of(key, extent, shards, -0.22, 0.18)
    return jnp.clip(with_spikes(entries, jax.random.fold_in(key, 3), *heavy), -reach, reach).astype(held_as)


def setup_inputs(seed: int = 0) -> dict:
    splits = jax.random.split(jax.random.key(seed), 7)
    return {
        "normed": noise_with(splits[0], (SEQUENCE_COUNT, SEQUENCE_LENGTH, D), 1.0, 6.0, ((0, 8), (1, 4)), (1, 2, 4, 2.0)),
        "queries": draw_queries(jax.random.fold_in(splits[6], 71), 0),
        "keys": draw_keys(jax.random.fold_in(splits[6], 71), 0),
        "values": gaussian(splits[3], (SEQUENCE_COUNT, SEQUENCE_LENGTH, KEY_VALUE_HEADS * HEAD_SIZE), 1.0, 6.0, ((0, 8), (1, 4))),
        "out_grad": gaussian(splits[4], (SEQUENCE_COUNT, SEQUENCE_LENGTH, QUERY_HEADS * HEAD_SIZE), 24.0, 150.0, ((0, 8), (1, 4))),
        "segment_ids": jax.vmap(lambda own: jnp.searchsorted(jnp.cumsum(uneven_parts(own, DOCS, SEQUENCE_LENGTH, 3 * SEQUENCE_LENGTH // 4, 1)), jnp.arange(SEQUENCE_LENGTH), side="right"))(jax.random.split(splits[5], SEQUENCE_COUNT)).reshape((SEQUENCE_COUNT, SEQUENCE_LENGTH)).astype(jnp.int32),
    }


query_scalar = 168.0


def band_core(queries, keys, values, out_grad, allowed):
    count = queries.shape[0]
    span = keys.shape[0]
    groups = keys.shape[1] // HEAD_SIZE
    ratio = queries.shape[1] // keys.shape[1]
    softmax_scale = query_scalar ** -0.5
    matmul_precision_mode = lax.Precision.HIGHEST
    query_head_rows = queries.reshape(count, groups, ratio, HEAD_SIZE).astype(jnp.float32)
    key_head_rows = keys.reshape(span, groups, HEAD_SIZE).astype(jnp.float32)
    value_head_rows = values.reshape(span, groups, HEAD_SIZE).astype(jnp.float32)
    head_gradient = out_grad.reshape(count, groups, ratio, HEAD_SIZE).astype(jnp.float32)
    attention_scores = jnp.einsum("qczw,jcw->czqj", query_head_rows, key_head_rows, precision=matmul_precision_mode) * softmax_scale
    attention_scores = jnp.where(allowed[None, None], attention_scores, -jnp.inf)
    highest = jnp.max(attention_scores, axis=-1, keepdims=True)
    expanded = jnp.exp(attention_scores - highest)
    weights_full = expanded / jnp.sum(expanded, axis=-1, keepdims=True)
    reduced_precision_weight = weights_full.astype(jnp.bfloat16).astype(jnp.float32)
    attention_output = jnp.einsum("mlhv,vmo->mlho", reduced_precision_weight, value_head_rows, precision=matmul_precision_mode)
    grad_major = jnp.transpose(head_gradient, (1, 2, 0, 3))
    delta = jnp.sum(grad_major * attention_output, axis=-1, keepdims=True)
    probability_gradient = jnp.einsum("qczw,jcw->czqj", head_gradient, value_head_rows, precision=matmul_precision_mode)
    score_gradient = (weights_full * (probability_gradient - delta)).astype(jnp.bfloat16).astype(jnp.float32)
    query_gradient = jnp.einsum("fwcj,jfe->cfwe", score_gradient, key_head_rows, precision=matmul_precision_mode) * softmax_scale
    key_gradient = jnp.einsum("vbzp,zvba->pva", score_gradient, query_head_rows, precision=matmul_precision_mode) * softmax_scale
    value_gradient = jnp.einsum("vbzp,zvba->pva", reduced_precision_weight, head_gradient, precision=matmul_precision_mode)
    return (query_gradient.reshape(count, -1).astype(jnp.bfloat16),
            key_gradient.reshape(span, -1).astype(jnp.bfloat16),
            value_gradient.reshape(span, -1).astype(jnp.bfloat16))


def one_sequence(inputs):
    queries, keys, values, out_grad, segment_ids = inputs
    width = keys.shape[1]
    span = WINDOW + TOK_DEV
    key_pad = jnp.concatenate([jnp.zeros((WINDOW, width), keys.dtype), keys], axis=0)
    value_pad = jnp.concatenate([jnp.zeros((WINDOW, width), values.dtype), values], axis=0)
    id_pad = jnp.concatenate([jnp.full((WINDOW,), -1, jnp.int32), segment_ids.astype(jnp.int32)])
    offsets = jnp.arange(TOK_DEV, dtype=jnp.int32)[:, None] - jnp.arange(span, dtype=jnp.int32)[None, :] + WINDOW

    def step(carry, index):
        key_total, value_total = carry
        start = (index * TOK_DEV).astype(jnp.int32)
        query_block = lax.dynamic_slice_in_dim(queries, start, TOK_DEV, 0)
        grad_block = lax.dynamic_slice_in_dim(out_grad, start, TOK_DEV, 0)
        key_block = lax.dynamic_slice_in_dim(key_pad, start, span, 0)
        value_block = lax.dynamic_slice_in_dim(value_pad, start, span, 0)
        query_ids = lax.dynamic_slice_in_dim(segment_ids.astype(jnp.int32), start, TOK_DEV, 0)
        key_ids = lax.dynamic_slice_in_dim(id_pad, start, span, 0)
        allowed = (query_ids[:, None] == key_ids[None, :]) & (offsets >= 0) & (offsets < WINDOW)
        query_gradient, key_gradient, value_gradient = band_core(query_block, key_block, value_block, grad_block, allowed)
        key_total = lax.dynamic_update_slice_in_dim(
            key_total, lax.dynamic_slice_in_dim(key_total, start, span, 0) + key_gradient.astype(jnp.float32), start, 0)
        value_total = lax.dynamic_update_slice_in_dim(
            value_total, lax.dynamic_slice_in_dim(value_total, start, span, 0) + value_gradient.astype(jnp.float32), start, 0)
        return (key_total, value_total), query_gradient

    zero_filled = jnp.zeros((WINDOW + SEQUENCE_LENGTH, width), jnp.float32)
    (key_total, value_total), query_gradient = lax.scan(step, (zero_filled, zero_filled), jnp.arange(N_CTX, dtype=jnp.int32))
    return (query_gradient.reshape(SEQUENCE_LENGTH, -1),
            key_total[WINDOW:].astype(jnp.bfloat16),
            value_total[WINDOW:].astype(jnp.bfloat16))


def reference(normed, queries, keys, values, out_grad, segment_ids):
    grad_queries, grad_keys, grad_values = lax.map(one_sequence, (queries, keys, values, out_grad, segment_ids))

    def sequence_step(total, pair):
        normed_seq, value_seq = pair
        input_blocks = normed_seq.reshape(N_CTX, TOK_DEV, -1)
        value_blocks = value_seq.reshape(N_CTX, TOK_DEV, -1)

        def block_step(running, block):
            term = jnp.dot(block[0].T, block[1], preferred_element_type=jnp.float32)
            return running + term.astype(jnp.bfloat16).astype(jnp.float32), None

        sequence_total, ignored = lax.scan(block_step, jnp.zeros_like(total), (input_blocks, value_blocks))
        return total + sequence_total.astype(jnp.bfloat16).astype(jnp.float32), None

    initial = jnp.zeros((normed.shape[2], values.shape[2]), jnp.float32)
    total, ignored = lax.scan(sequence_step, initial, (normed, grad_values))
    grad_weight = (total * (ALL_TOK ** -0.5)).astype(jnp.bfloat16)
    return grad_queries, grad_keys, grad_values, grad_weight
```

```python
import functools

import jax
import jax.numpy as jnp
from jax import lax
from jax.experimental import pallas as pl
from jax.experimental.pallas import tpu as pltpu
from jax.sharding import PartitionSpec as P

HEAD_SIZE = 128
WINDOW = 1024
MESH = pl.DeviceIdType.MESH

query_scalar = 168.0


def flipped(index, mask):
    bit = 1
    while bit <= mask:
        if mask & bit:
            index = index + bit - 2 * bit * lax.rem(index // bit, 2)
        bit *= 2
    return index


def row_step(rows):
    return max(s for s in range(16, 449, 16) if rows % s == 0)


def mm(a, b, ca, cb):
    return lax.dot_general(a, b, (((ca,), (cb,)), ((), ())), preferred_element_type=jnp.float32)


def kernel(
    cfg,
    normed_ref, q_ref, k_ref, v_ref, do_ref, ids_ref,
    dq_ref, dk_ref, dv_ref, dw_ref,
    kbuf, vbuf, dk_out, dv_out, dk_in, dv_in, own_dk, own_dv, bias,
    nbuf, gbuf, w_own, w_send, w_sib, r_send, r_up, r_down,
    kv_send, kv_recv, back_send, back_recv, n_send, n_recv, g_send, g_recv, s_send, s_recv,
    u_send, u_recv, d_send, d_recv,
):
    chain, nd, count, blocks, chunks, heads, ratio, window = cfg
    c = lax.axis_index("ctx")
    d = lax.axis_index("dp")
    chips = nd // 2
    m, core = d // 2, lax.rem(d, 2)
    wide = heads * HEAD_SIZE
    scale = query_scalar ** (-0.5)
    features = normed_ref.shape[1]
    has_next, has_prev = c < chain - 1, c > 0

    def chip_at(mask):
        return {"dp": flipped(m, mask) * 2 + core}

    sibling = {"dp": m * 2 + 1 - core}
    after, before = {"ctx": c + 1}, {"ctx": c - 1}

    barrier = pltpu.get_barrier_semaphore()

    @pl.when(has_next)
    def _():
        pl.semaphore_signal(barrier, inc=1, device_id=after, device_id_type=MESH)

    @pl.when(has_prev)
    def _():
        pl.semaphore_signal(barrier, inc=1, device_id=before, device_id_type=MESH)

    for r in range(1, chips):
        pl.semaphore_signal(barrier, inc=1, device_id=chip_at(r), device_id_type=MESH)
    pl.semaphore_signal(barrier, inc=1, device_id=sibling, device_id_type=MESH)

    for s in range(1, blocks):
        @pl.when(c < s)
        def _():
            kbuf[s - 1] = jnp.zeros_like(kbuf[s - 1])
            vbuf[s - 1] = jnp.zeros_like(vbuf[s - 1])

    own_ids = ids_ref[:, pl.ds(pl.multiple_of(c * count, count), count)]
    query_ids = jnp.transpose(jnp.broadcast_to(own_ids, (count, count)))
    row = lax.broadcasted_iota(jnp.int32, (count, count), 0)
    col = lax.broadcasted_iota(jnp.int32, (count, count), 1)
    for s in range(blocks):
        at = jnp.maximum(c - s, 0)
        key_ids = ids_ref[:, pl.ds(pl.multiple_of(at * count, count), count)]
        offset = row - col + s * count
        good = (query_ids == key_ids) & (offset >= 0) & (offset < window) & (offset <= c * count + row)
        bias[:, s * count : (s + 1) * count] = jnp.where(good, 0.0, -jnp.inf)

    pl.semaphore_wait(barrier, has_next.astype(jnp.int32) + has_prev.astype(jnp.int32) + chips)

    def remote(src, dst, send, recv, where):
        return pltpu.make_async_remote_copy(
            src_ref=src, dst_ref=dst, send_sem=send, recv_sem=recv, device_id=where, device_id_type=MESH
        )

    def kv_copy(h, s, i):
        cols = pl.ds(pl.multiple_of(h * wide, wide), wide)
        own, buf = ((k_ref, kbuf), (v_ref, vbuf))[i]
        return remote(
            (own if s == 1 else buf.at[s - 2]).at[:, cols], buf.at[s - 1].at[:, cols],
            kv_send.at[h, s - 1, i], kv_recv.at[h, s - 1, i], after,
        )

    def kv_copies(h, s):
        return [kv_copy(h, s, i) for i in range(2)]

    def back_copy(h, s, i):
        cols = pl.ds(pl.multiple_of(h * wide, wide), wide)
        src, dst = ((dv_out, dv_in), (dk_out, dk_in))[i]
        return remote(
            src.at[s - 1].at[:, cols], dst.at[s - 1].at[:, cols],
            back_send.at[h, s - 1, i], back_recv.at[h, s - 1, i], before,
        )

    def send_own(h):
        @pl.when(has_next)
        def _():
            for copy in kv_copies(h, 1):
                copy.start()

    def forward(h):
        for s in range(1, blocks):
            @pl.when(c >= s)
            def _():
                for copy in kv_copies(h, s):
                    copy.wait_recv()

            if s + 1 < blocks:
                @pl.when((c >= s) & has_next)
                def _():
                    for copy in kv_copies(h, s + 1):
                        copy.start()

    half = (features // 256) * 128
    parts = ((0, half), (half, features - half))

    def n_copy(r, part, src, to):
        lo, size = parts[part]
        return remote(
            src.at[:, lo : lo + size], nbuf.at[r - 1].at[:, lo : lo + size],
            n_send.at[r - 1, part], n_recv.at[r - 1, part], chip_at(to),
        )

    relay = chips == 4

    def n_first():
        if relay:
            for r, part in ((1, 0), (2, 1), (1, 1), (2, 0)):
                n_copy(r, part, normed_ref, r).start()
        else:
            for r in range(1, chips):
                for part in range(2):
                    n_copy(r, part, normed_ref, r).start()

    def n_relay():
        if relay:
            n_copy(1, 0, normed_ref, 1).wait_recv()
            n_copy(3, 0, nbuf.at[0], 2).start()
            n_copy(2, 1, normed_ref, 2).wait_recv()
            n_copy(3, 1, nbuf.at[1], 1).start()

    def n_finish():
        for r in range(1, chips):
            for part in range(2):
                copy = n_copy(r, part, normed_ref, r)
                if not (relay and (r, part) in ((1, 0), (2, 1))):
                    copy.wait_recv()
                copy.wait_send()

    def compute(h):
        for g in range(heads):
            head = h * heads + g
            kv_cols = pl.ds(pl.multiple_of(head * HEAD_SIZE, HEAD_SIZE), HEAD_SIZE)

            def stacked(ref):
                return jnp.concatenate(
                    [
                        ref[:, pl.ds(pl.multiple_of((head * ratio + z) * HEAD_SIZE, HEAD_SIZE), HEAD_SIZE)]
                        for z in range(ratio)
                    ],
                    axis=0,
                )

            q, do = stacked(q_ref), stacked(do_ref)
            keys = jnp.concatenate([k_ref[:, kv_cols]] + [kbuf[s - 1, :, kv_cols] for s in range(1, blocks)], axis=0)
            values = jnp.concatenate([v_ref[:, kv_cols]] + [vbuf[s - 1, :, kv_cols] for s in range(1, blocks)], axis=0)
            scores = mm(q, keys, 1, 1) * scale
            scores = scores + jnp.concatenate([bias[...]] * ratio, axis=0)
            top = jnp.max(scores, axis=1, keepdims=True)
            expanded = jnp.exp(scores - top)
            weights = expanded * (1.0 / jnp.sum(expanded, axis=1, keepdims=True))
            low = weights.astype(jnp.bfloat16)
            grad_probs = mm(do, values, 1, 1)
            delta = jnp.sum(low.astype(jnp.float32) * grad_probs, axis=1, keepdims=True)
            grad_scores = (weights * (grad_probs - delta)).astype(jnp.bfloat16)
            dq = (mm(grad_scores, keys, 1, 0) * scale).astype(jnp.bfloat16)
            for z in range(ratio):
                dq_ref[:, pl.ds(pl.multiple_of((head * ratio + z) * HEAD_SIZE, HEAD_SIZE), HEAD_SIZE)] = dq[
                    z * count : (z + 1) * count
                ]
            dv = mm(low, do, 0, 0)
            dk = mm(grad_scores, q, 0, 0) * scale
            for s in range(blocks):
                own_dv[s, :, kv_cols] = dv[s * count : (s + 1) * count]
                own_dk[s, :, kv_cols] = dk[s * count : (s + 1) * count]

    def give_back(h, last, which):
        cols = pl.ds(pl.multiple_of(h * wide, wide), wide)
        own, into, out, final = ((own_dv, dv_in, dv_out, dv_ref), (own_dk, dk_in, dk_out, dk_ref))[which]
        for s in range(blocks - 1, -1, -1):
            takes = not last and s + 1 < blocks

            def total():
                value = own[s, :, cols]
                if takes:
                    value = value + into[s, :, cols].astype(jnp.float32)
                return value.astype(jnp.bfloat16)

            if s > 0:
                @pl.when(c >= s)
                def _():
                    if takes:
                        back_copy(h, s + 1, which).wait_recv()
                    out[s - 1, :, cols] = total()
                    back_copy(h, s, which).start()
            else:
                if takes:
                    back_copy(h, 1, which).wait_recv()
                final[:, cols] = total()

    send_own(0)
    if chunks > 1:
        send_own(1)
    n_first()
    forward(0)

    def chunk(h, carry):
        compute(h)

        @pl.when((c == chain - 1) & (h < chunks - 1))
        def _():
            give_back(h, True, 0)
            give_back(h, True, 1)

        @pl.when(h + 2 < chunks)
        def _():
            send_own(h + 2)

        @pl.when(h + 1 < chunks)
        def _():
            forward(h + 1)

        @pl.when(has_next & (h < chunks - 1))
        def _():
            give_back(h, False, 0)
            give_back(h, False, 1)

        @pl.when(h == min(1, chunks - 1))
        def _():
            n_relay()

        return carry

    lax.fori_loop(0, chunks, chunk, 0)

    end = chunks - 1

    @pl.when(c == chain - 1)
    def _():
        give_back(end, True, 0)
        give_back(end, True, 1)

    @pl.when(has_next)
    def _():
        give_back(end, False, 0)

    pair = gbuf.shape[2]
    cw = pair // 2

    def g_copy(r):
        to = flipped(m, r)
        return remote(
            dv_ref.at[:, pl.ds(pl.multiple_of(to * pair, pair), pair)], gbuf.at[r - 1],
            g_send.at[r - 1], g_recv.at[r - 1], chip_at(r),
        )

    for r in range(1, chips):
        g_copy(r).start()

    @pl.when(has_next)
    def _():
        give_back(end, False, 1)

    n_finish()
    for r in range(1, chips):
        g_copy(r).wait_recv()

    own_g = dv_ref[:, pl.ds(pl.multiple_of(m * pair, pair), pair)]
    tile = 384 if features % 384 == 0 else 128

    def w_tile(t, carry):
        cols = pl.ds(pl.multiple_of(t * tile, tile), tile)
        acc = mm(normed_ref[:, cols], own_g, 0, 0)
        for r in range(1, chips):
            acc = acc + mm(nbuf[r - 1, :, cols], gbuf[r - 1], 0, 0)
        low = acc[:, :cw]
        high = acc[:, cw:] if cw % 128 == 0 else pltpu.roll(acc, cw, 1)[:, :cw]
        first = core == 0
        w_own[cols, :] = jnp.where(first, low, high)
        w_send[cols, :] = jnp.where(first, high, low).astype(jnp.bfloat16)
        return carry

    lax.fori_loop(0, features // tile, w_tile, 0)

    rows = features // chain

    def s_copy(r):
        span = pl.ds(r * rows, rows)
        return remote(w_send.at[span], w_sib.at[span], s_send.at[r], s_recv.at[r], sibling)

    order = []
    for t in range(chain):
        order += [chain - 1 - t, t]
    order = list(dict.fromkeys(order))
    for r in order:
        s_copy(r).start()

    step = row_step(rows)

    def u_copy(r):
        return remote(r_send.at[r], r_up.at[r], u_send.at[r], u_recv.at[r], after)

    def d_copy(r):
        return remote(r_send.at[r], r_down.at[r], d_send.at[r], d_recv.at[r], before)

    def sums(r, extra, put):
        def one(t, carry):
            lo = pl.multiple_of(t * step, step)
            base = pl.ds(pl.multiple_of(r * rows + t * step, 16), step)
            value = w_own[base, :] + w_sib[base, :].astype(jnp.float32)
            for ref in extra:
                value = value + ref[r, pl.ds(lo, step), :].astype(jnp.float32)
            put(pl.ds(lo, step), value)
            return carry

        lax.fori_loop(0, rows // step, one, 0)

    def put_send(r):
        def put(span, value):
            r_send[r, span, :] = value.astype(jnp.bfloat16)
        return put

    arrived = set()

    def sib_ready(r):
        if r not in arrived:
            arrived.add(r)
            s_copy(r).wait_recv()

    def up_piece(r):
        @pl.when(c == 0)
        def _():
            sums(r, (), put_send(r))
            u_copy(r).start()

        @pl.when((c > 0) & (c < r))
        def _():
            u_copy(r).wait_recv()
            sums(r, (r_up,), put_send(r))
            u_copy(r).start()

    def down_piece(r):
        @pl.when(c == chain - 1)
        def _():
            sums(r, (), put_send(r))
            d_copy(r).start()

        @pl.when((c < chain - 1) & (c > r))
        def _():
            d_copy(r).wait_recv()
            sums(r, (r_down,), put_send(r))
            d_copy(r).start()

    for t in range(chain - 1):
        sib_ready(chain - 1 - t)
        up_piece(chain - 1 - t)
        sib_ready(t)
        down_piece(t)
    for r in range(chain):
        sib_ready(r)

    final_scale = (count * chain * nd) ** (-0.5)

    def put_final(span, value):
        dw_ref[span, :] = (value * final_scale).astype(jnp.bfloat16)

    @pl.when(has_prev)
    def _():
        u_copy(c).wait_recv()

    @pl.when(has_next)
    def _():
        d_copy(c).wait_recv()

    @pl.when(c == 0)
    def _():
        sums(c, (r_down,), put_final)

    @pl.when(c == chain - 1)
    def _():
        sums(c, (r_up,), put_final)

    @pl.when(has_prev & has_next)
    def _():
        sums(c, (r_up, r_down), put_final)

    def drain(h, carry):
        for s in range(1, blocks):
            @pl.when(has_next & (c >= s - 1))
            def _():
                for copy in kv_copies(h, s):
                    copy.wait_send()

            @pl.when(c >= s)
            def _():
                for i in range(2):
                    back_copy(h, s, i).wait_send()
        return carry

    lax.fori_loop(0, chunks, drain, 0)
    for r in range(1, chips):
        g_copy(r).wait_send()
    for r in range(chain):
        s_copy(r).wait_send()

        @pl.when(c < r)
        def _():
            u_copy(r).wait_send()

        @pl.when(c > r)
        def _():
            d_copy(r).wait_send()


def body(normed, queries, keys, values, out_grad, segment_ids):
    count = queries.shape[1]
    width = keys.shape[2]
    features = normed.shape[2]
    chain, nd = lax.axis_size("ctx"), lax.axis_size("dp")
    chips = nd // 2
    blocks = min(-(-WINDOW // count), chain - 1) + 1
    groups = width // HEAD_SIZE
    heads = max(1, groups // 4)
    chunks = groups // heads
    ratio = queries.shape[2] // width
    cw = width // nd
    rows = features // chain
    bf, f32 = jnp.bfloat16, jnp.float32
    vm = pltpu.VMEM
    dma = pltpu.SemaphoreType.DMA
    back = blocks - 1
    cfg = (chain, nd, count, blocks, chunks, heads, ratio, WINDOW)
    out = pl.pallas_call(
        functools.partial(kernel, cfg),
        out_shape=(
            jax.ShapeDtypeStruct(queries.shape[1:], bf),
            jax.ShapeDtypeStruct(keys.shape[1:], bf),
            jax.ShapeDtypeStruct(keys.shape[1:], bf),
            jax.ShapeDtypeStruct((rows, cw), bf),
        ),
        in_specs=[pl.BlockSpec(memory_space=vm)] * 6,
        out_specs=(pl.BlockSpec(memory_space=vm),) * 4,
        scratch_shapes=[
            vm((back, count, width), bf), vm((back, count, width), bf),
            vm((back, count, width), bf), vm((back, count, width), bf),
            vm((back, count, width), bf), vm((back, count, width), bf),
            vm((blocks, count, width), f32), vm((blocks, count, width), f32),
            vm((count, blocks * count), f32),
            vm((chips - 1, count, features), bf), vm((chips - 1, count, 2 * cw), bf),
            vm((features, cw), f32), vm((features, cw), bf), vm((features, cw), bf),
            vm((chain, rows, cw), bf), vm((chain, rows, cw), bf), vm((chain, rows, cw), bf),
            dma((chunks, back, 2)), dma((chunks, back, 2)), dma((chunks, back, 2)), dma((chunks, back, 2)),
            dma((chips - 1, 2)), dma((chips - 1, 2)), dma((chips - 1,)), dma((chips - 1,)),
            dma((chain,)), dma((chain,)), dma((chain,)), dma((chain,)), dma((chain,)), dma((chain,)),
        ],
        compiler_params=pltpu.CompilerParams(
            collective_id=0, has_side_effects=True, vmem_limit_bytes=64000 * 1024
        ),
    )(normed[0], queries[0], keys[0], values[0], out_grad[0], segment_ids)
    return out[0][None], out[1][None], out[2][None], out[3]


def solution(mesh):
    placed = (P("dp", "ctx", None),) * 5 + (P("dp", None),)
    return jax.shard_map(
        body,
        mesh=mesh,
        in_specs=placed,
        out_specs=(
            P("dp", "ctx", None),
            P("dp", "ctx", None),
            P("dp", "ctx", None),
            P("ctx", "dp"),
        ),
        check_vma=False,
    )
```

```python
import functools

import jax
import jax.numpy as jnp
from jax import lax
from jax.experimental import pallas as pl
from jax.experimental.pallas import tpu as pltpu
from jax.sharding import PartitionSpec as P

HEAD_SIZE = 128
WINDOW = 1024
MESH = pl.DeviceIdType.MESH

query_scalar = 168.0


def flipped(index, mask):
    bit = 1
    while bit <= mask:
        if mask & bit:
            index = index + bit - 2 * bit * lax.rem(index // bit, 2)
        bit *= 2
    return index


def mm(a, b, ca, cb):
    return lax.dot_general(a, b, (((ca,), (cb,)), ((), ())), preferred_element_type=jnp.float32)


def kernel(
    cfg,
    normed_ref, q_ref, k_ref, v_ref, do_ref, ids_ref,
    dq_ref, dk_ref, dv_ref, dw_ref,
    kbuf, vbuf, dk_out, dv_out, dk_in, dv_in, own_dk, own_dv, bias,
    nbuf, gbuf, w_own, w_send, w_sib, r_send, r_up, r_down,
    kv_send, kv_recv, back_send, back_recv, n_send, n_recv, g_send, g_recv, s_send, s_recv,
    u_send, u_recv, d_send, d_recv,
):
    chain, nd, count, blocks, chunks, heads, ratio, window = cfg
    c = lax.axis_index("ctx")
    d = lax.axis_index("dp")
    chips = nd // 2
    m, core = d // 2, lax.rem(d, 2)
    wide = heads * HEAD_SIZE
    scale = query_scalar ** (-0.5)
    features = normed_ref.shape[1]
    has_next, has_prev = c < chain - 1, c > 0

    def chip_at(mask):
        return {"dp": flipped(m, mask) * 2 + core}

    sibling = {"dp": m * 2 + 1 - core}
    after, before = {"ctx": c + 1}, {"ctx": c - 1}

    barrier = pltpu.get_barrier_semaphore()

    @pl.when(has_next)
    def _():
        pl.semaphore_signal(barrier, inc=1, device_id=after, device_id_type=MESH)

    @pl.when(has_prev)
    def _():
        pl.semaphore_signal(barrier, inc=1, device_id=before, device_id_type=MESH)

    for r in range(1, chips):
        pl.semaphore_signal(barrier, inc=1, device_id=chip_at(r), device_id_type=MESH)
    pl.semaphore_signal(barrier, inc=1, device_id=sibling, device_id_type=MESH)

    for s in range(1, blocks):
        @pl.when(c < s)
        def _():
            kbuf[s - 1] = jnp.zeros_like(kbuf[s - 1])
            vbuf[s - 1] = jnp.zeros_like(vbuf[s - 1])

    own_ids = ids_ref[:, pl.ds(pl.multiple_of(c * count, count), count)]
    query_ids = jnp.transpose(jnp.broadcast_to(own_ids, (count, count)))
    row = lax.broadcasted_iota(jnp.int32, (count, count), 0)
    col = lax.broadcasted_iota(jnp.int32, (count, count), 1)
    for s in range(blocks):
        at = jnp.maximum(c - s, 0)
        key_ids = ids_ref[:, pl.ds(pl.multiple_of(at * count, count), count)]
        offset = row - col + s * count
        good = (query_ids == key_ids) & (offset >= 0) & (offset < window) & (offset <= c * count + row)
        bias[:, s * count : (s + 1) * count] = jnp.where(good, 0.0, -jnp.inf)

    pl.semaphore_wait(barrier, has_next.astype(jnp.int32) + has_prev.astype(jnp.int32) + chips)

    def remote(src, dst, send, recv, where):
        return pltpu.make_async_remote_copy(
            src_ref=src, dst_ref=dst, send_sem=send, recv_sem=recv, device_id=where, device_id_type=MESH
        )

    def kv_copy(h, s, i):
        cols = pl.ds(pl.multiple_of(h * wide, wide), wide)
        own, buf = ((k_ref, kbuf), (v_ref, vbuf))[i]
        return remote(
            (own if s == 1 else buf.at[s - 2]).at[:, cols], buf.at[s - 1].at[:, cols],
            kv_send.at[h, s - 1, i], kv_recv.at[h, s - 1, i], after,
        )

    def kv_copies(h, s):
        return [kv_copy(h, s, i) for i in range(2)]

    def back_copy(h, s, i):
        cols = pl.ds(pl.multiple_of(h * wide, wide), wide)
        src, dst = ((dv_out, dv_in), (dk_out, dk_in))[i]
        return remote(
            src.at[s - 1].at[:, cols], dst.at[s - 1].at[:, cols],
            back_send.at[h, s - 1, i], back_recv.at[h, s - 1, i], before,
        )

    def send_own(h):
        @pl.when(has_next)
        def _():
            for copy in kv_copies(h, 1):
                copy.start()

    def forward(h):
        for s in range(1, blocks):
            @pl.when(c >= s)
            def _():
                for copy in kv_copies(h, s):
                    copy.wait_recv()

            if s + 1 < blocks:
                @pl.when((c >= s) & has_next)
                def _():
                    for copy in kv_copies(h, s + 1):
                        copy.start()

    half = (features // 256) * 128
    parts = ((0, half), (half, features - half))

    def n_copy(r, part, src, to):
        lo, size = parts[part]
        return remote(
            src.at[:, lo : lo + size], nbuf.at[r - 1].at[:, lo : lo + size],
            n_send.at[r - 1, part], n_recv.at[r - 1, part], chip_at(to),
        )

    relay = chips == 4

    def n_first():
        if relay:
            for r, part in ((1, 0), (2, 1), (1, 1), (2, 0)):
                n_copy(r, part, normed_ref, r).start()
        else:
            for r in range(1, chips):
                for part in range(2):
                    n_copy(r, part, normed_ref, r).start()

    def n_relay():
        if relay:
            n_copy(1, 0, normed_ref, 1).wait_recv()
            n_copy(3, 0, nbuf.at[0], 2).start()
            n_copy(2, 1, normed_ref, 2).wait_recv()
            n_copy(3, 1, nbuf.at[1], 1).start()

    def n_finish():
        for r in range(1, chips):
            for part in range(2):
                copy = n_copy(r, part, normed_ref, r)
                if not (relay and (r, part) in ((1, 0), (2, 1))):
                    copy.wait_recv()
                copy.wait_send()

    def compute(h):
        for g in range(heads):
            head = h * heads + g
            kv_cols = pl.ds(pl.multiple_of(head * HEAD_SIZE, HEAD_SIZE), HEAD_SIZE)

            def stacked(ref):
                return jnp.concatenate(
                    [
                        ref[:, pl.ds(pl.multiple_of((head * ratio + z) * HEAD_SIZE, HEAD_SIZE), HEAD_SIZE)]
                        for z in range(ratio)
                    ],
                    axis=0,
                )

            q, do = stacked(q_ref), stacked(do_ref)
            keys = jnp.concatenate([k_ref[:, kv_cols]] + [kbuf[s - 1, :, kv_cols] for s in range(1, blocks)], axis=0)
            values = jnp.concatenate([v_ref[:, kv_cols]] + [vbuf[s - 1, :, kv_cols] for s in range(1, blocks)], axis=0)
            scores = mm(q, keys, 1, 1) * scale
            scores = scores + jnp.concatenate([bias[...]] * ratio, axis=0)
            top = jnp.max(scores, axis=1, keepdims=True)
            expanded = jnp.exp(scores - top)
            weights = expanded * (1.0 / jnp.sum(expanded, axis=1, keepdims=True))
            low = weights.astype(jnp.bfloat16)
            grad_probs = mm(do, values, 1, 1)
            delta = jnp.sum(low.astype(jnp.float32) * grad_probs, axis=1, keepdims=True)
            grad_scores = (weights * (grad_probs - delta)).astype(jnp.bfloat16)
            dq = (mm(grad_scores, keys, 1, 0) * scale).astype(jnp.bfloat16)
            for z in range(ratio):
                dq_ref[:, pl.ds(pl.multiple_of((head * ratio + z) * HEAD_SIZE, HEAD_SIZE), HEAD_SIZE)] = dq[
                    z * count : (z + 1) * count
                ]
            dv = mm(low, do, 0, 0)
            dk = mm(grad_scores, q, 0, 0) * scale
            for s in range(blocks):
                own_dv[s, :, kv_cols] = dv[s * count : (s + 1) * count]
                own_dk[s, :, kv_cols] = dk[s * count : (s + 1) * count]

    def give_back(h, last, which):
        cols = pl.ds(pl.multiple_of(h * wide, wide), wide)
        own, into, out, final = ((own_dv, dv_in, dv_out, dv_ref), (own_dk, dk_in, dk_out, dk_ref))[which]
        for s in range(blocks - 1, -1, -1):
            takes = not last and s + 1 < blocks

            def total():
                value = own[s, :, cols]
                if takes:
                    value = value + into[s, :, cols].astype(jnp.float32)
                return value.astype(jnp.bfloat16)

            if s > 0:
                @pl.when(c >= s)
                def _():
                    if takes:
                        back_copy(h, s + 1, which).wait_recv()
                    out[s - 1, :, cols] = total()
                    back_copy(h, s, which).start()
            else:
                if takes:
                    back_copy(h, 1, which).wait_recv()
                final[:, cols] = total()

    lag = jnp.where(c == chain - 1, 0, jnp.where(c == chain - 2, min(2, chunks), chunks))
    end = chunks - 1
    send_own(0)
    if chunks > 1:
        send_own(1)
    n_first()

    def chunk(i, carry):
        @pl.when(i < chunks)
        def _():
            forward(i)

            @pl.when(i + 2 < chunks)
            def _():
                send_own(i + 2)

            compute(i)

        j = i - lag
        turn = (j >= 0) & (j < end)

        @pl.when(turn & (c == chain - 1))
        def _():
            give_back(j, True, 0)
            give_back(j, True, 1)

        @pl.when(turn & has_next)
        def _():
            give_back(j, False, 0)
            give_back(j, False, 1)

        @pl.when(i == min(2, end))
        def _():
            n_relay()

        return carry

    lax.fori_loop(0, 2 * chunks, chunk, 0)

    @pl.when(c == chain - 1)
    def _():
        give_back(end, True, 0)
        give_back(end, True, 1)

    @pl.when(has_next)
    def _():
        give_back(end, False, 0)

    pair = gbuf.shape[2]
    cw = pair // 2

    def g_copy(r):
        to = flipped(m, r)
        return remote(
            dv_ref.at[:, pl.ds(pl.multiple_of(to * pair, pair), pair)], gbuf.at[r - 1],
            g_send.at[r - 1], g_recv.at[r - 1], chip_at(r),
        )

    for r in range(1, chips):
        g_copy(r).start()

    @pl.when(has_next)
    def _():
        give_back(end, False, 1)

    n_finish()
    for r in range(1, chips):
        g_copy(r).wait_recv()

    own_g = dv_ref[:, pl.ds(pl.multiple_of(m * pair, pair), pair)]
    tile = 384 if features % 384 == 0 else 128

    def w_tile(t, carry):
        cols = pl.ds(pl.multiple_of(t * tile, tile), tile)
        acc = mm(normed_ref[:, cols], own_g, 0, 0)
        for r in range(1, chips):
            acc = acc + mm(nbuf[r - 1, :, cols], gbuf[r - 1], 0, 0)
        low = acc[:, :cw]
        high = acc[:, cw:] if cw % 128 == 0 else pltpu.roll(acc, cw, 1)[:, :cw]
        first = core == 0
        w_own[cols, :] = jnp.where(first, low, high)
        w_send[cols, :] = jnp.where(first, high, low).astype(jnp.bfloat16)
        return carry

    lax.fori_loop(0, features // tile, w_tile, 0)

    rows = features // chain
    subs = r_send.shape[0] // chain
    step = rows // subs
    whole = chain * subs

    def s_copy(p):
        span = pl.ds(pl.multiple_of(p * step, 16), step)
        return remote(w_send.at[span], w_sib.at[span], s_send.at[p], s_recv.at[p], sibling)

    def u_copy(p):
        return remote(r_send.at[p], r_up.at[p], u_send.at[p], u_recv.at[p], after)

    def d_copy(p):
        return remote(r_send.at[p], r_down.at[p], d_send.at[p], d_recv.at[p], before)

    def up_index(u):
        return (chain - 1 - u // subs) * subs + lax.rem(u, subs)

    def send_sib(t, carry):
        flip = jnp.where(c < chain - c, up_index(t), t)
        s_copy(flip).start()
        return carry

    lax.fori_loop(0, whole, send_sib, 0)

    def sums(p, extra):
        base = pl.ds(pl.multiple_of(p * step, 16), step)
        value = w_own[base, :] + w_sib[base, :].astype(jnp.float32)
        for ref in extra:
            value = value + ref[p].astype(jnp.float32)
        return value

    def reduce_step(tau, carry):
        u = tau - 2 * c
        v = tau - 2 * (chain - 1 - c)

        @pl.when((u >= 0) & (u < (chain - 1 - c) * subs))
        def _():
            p = up_index(u)
            s_copy(p).wait_recv()

            @pl.when(c == 0)
            def _():
                r_send[p] = sums(p, ()).astype(jnp.bfloat16)

            @pl.when(c > 0)
            def _():
                u_copy(p).wait_recv()
                r_send[p] = sums(p, (r_up,)).astype(jnp.bfloat16)

            u_copy(p).start()

        @pl.when((v >= 0) & (v < c * subs))
        def _():
            s_copy(v).wait_recv()

            @pl.when(c == chain - 1)
            def _():
                r_send[v] = sums(v, ()).astype(jnp.bfloat16)

            @pl.when(c < chain - 1)
            def _():
                d_copy(v).wait_recv()
                r_send[v] = sums(v, (r_down,)).astype(jnp.bfloat16)

            d_copy(v).start()

        return carry

    lax.fori_loop(0, (chain - 1) * (subs + 2), reduce_step, 0)

    final_scale = (count * chain * nd) ** (-0.5)

    def finish(t, carry):
        p = c * subs + t
        s_copy(p).wait_recv()
        span = pl.ds(pl.multiple_of(t * step, 16), step)

        @pl.when(has_prev)
        def _():
            u_copy(p).wait_recv()

        @pl.when(has_next)
        def _():
            d_copy(p).wait_recv()

        @pl.when(c == 0)
        def _():
            dw_ref[span, :] = (sums(p, (r_down,)) * final_scale).astype(jnp.bfloat16)

        @pl.when(c == chain - 1)
        def _():
            dw_ref[span, :] = (sums(p, (r_up,)) * final_scale).astype(jnp.bfloat16)

        @pl.when(has_prev & has_next)
        def _():
            dw_ref[span, :] = (sums(p, (r_up, r_down)) * final_scale).astype(jnp.bfloat16)

        return carry

    lax.fori_loop(0, subs, finish, 0)

    def drain(h, carry):
        for s in range(1, blocks):
            @pl.when(has_next & (c >= s - 1))
            def _():
                for copy in kv_copies(h, s):
                    copy.wait_send()

            @pl.when(c >= s)
            def _():
                for i in range(2):
                    back_copy(h, s, i).wait_send()
        return carry

    lax.fori_loop(0, chunks, drain, 0)
    for r in range(1, chips):
        g_copy(r).wait_send()

    def drain_pieces(p, carry):
        s_copy(p).wait_send()

        @pl.when(p >= (c + 1) * subs)
        def _():
            u_copy(p).wait_send()

        @pl.when(p < c * subs)
        def _():
            d_copy(p).wait_send()

        return carry

    lax.fori_loop(0, whole, drain_pieces, 0)


def body(normed, queries, keys, values, out_grad, segment_ids):
    count = queries.shape[1]
    width = keys.shape[2]
    features = normed.shape[2]
    chain, nd = lax.axis_size("ctx"), lax.axis_size("dp")
    chips = nd // 2
    blocks = min(-(-WINDOW // count), chain - 1) + 1
    groups = width // HEAD_SIZE
    heads = max(1, groups // 4)
    chunks = groups // heads
    ratio = queries.shape[2] // width
    cw = width // nd
    rows = features // chain
    subs = max(n for n in range(1, 5) if rows % (16 * n) == 0)
    pieces = chain * subs
    bf, f32 = jnp.bfloat16, jnp.float32
    vm = pltpu.VMEM
    dma = pltpu.SemaphoreType.DMA
    back = blocks - 1
    cfg = (chain, nd, count, blocks, chunks, heads, ratio, WINDOW)
    out = pl.pallas_call(
        functools.partial(kernel, cfg),
        out_shape=(
            jax.ShapeDtypeStruct(queries.shape[1:], bf),
            jax.ShapeDtypeStruct(keys.shape[1:], bf),
            jax.ShapeDtypeStruct(keys.shape[1:], bf),
            jax.ShapeDtypeStruct((rows, cw), bf),
        ),
        in_specs=[pl.BlockSpec(memory_space=vm)] * 6,
        out_specs=(pl.BlockSpec(memory_space=vm),) * 4,
        scratch_shapes=[
            vm((back, count, width), bf), vm((back, count, width), bf),
            vm((back, count, width), bf), vm((back, count, width), bf),
            vm((back, count, width), bf), vm((back, count, width), bf),
            vm((blocks, count, width), f32), vm((blocks, count, width), f32),
            vm((count, blocks * count), f32),
            vm((chips - 1, count, features), bf), vm((chips - 1, count, 2 * cw), bf),
            vm((features, cw), f32), vm((features, cw), bf), vm((features, cw), bf),
            vm((pieces, rows // subs, cw), bf), vm((pieces, rows // subs, cw), bf), vm((pieces, rows // subs, cw), bf),
            dma((chunks, back, 2)), dma((chunks, back, 2)), dma((chunks, back, 2)), dma((chunks, back, 2)),
            dma((chips - 1, 2)), dma((chips - 1, 2)), dma((chips - 1,)), dma((chips - 1,)),
            dma((pieces,)), dma((pieces,)), dma((pieces,)), dma((pieces,)), dma((pieces,)), dma((pieces,)),
        ],
        compiler_params=pltpu.CompilerParams(
            collective_id=0, has_side_effects=True, vmem_limit_bytes=64000 * 1024
        ),
    )(normed[0], queries[0], keys[0], values[0], out_grad[0], segment_ids)
    return out[0][None], out[1][None], out[2][None], out[3]


def solution(mesh):
    placed = (P("dp", "ctx", None),) * 5 + (P("dp", None),)
    return jax.shard_map(
        body,
        mesh=mesh,
        in_specs=placed,
        out_specs=(
            P("dp", "ctx", None),
            P("dp", "ctx", None),
            P("dp", "ctx", None),
            P("ctx", "dp"),
        ),
        check_vma=False,
    )
```

```python
import functools

import jax
import jax.numpy as jnp
from jax import lax
from jax.experimental import pallas as pl
from jax.experimental.pallas import tpu as pltpu
from jax.sharding import PartitionSpec as P

HEAD_SIZE = 128
WINDOW = 1024
MESH = pl.DeviceIdType.MESH

query_scalar = 168.0


def flipped(index, mask):
    bit = 1
    while bit <= mask:
        if mask & bit:
            index = index + bit - 2 * bit * lax.rem(index // bit, 2)
        bit *= 2
    return index


def mm(a, b, ca, cb):
    return lax.dot_general(a, b, (((ca,), (cb,)), ((), ())), preferred_element_type=jnp.float32)


def kernel(
    cfg,
    normed_ref, q_ref, k_ref, v_ref, do_ref, ids_ref,
    dq_ref, dk_ref, dv_ref, dw_ref,
    kbuf, vbuf, dk_out, dv_out, dk_in, dv_in, own_dk, own_dv, bias,
    nbuf, gbuf, turned, w_own, w_send, w_sib, r_send, r_up, r_down,
    kv_send, kv_recv, back_send, back_recv, n_send, n_recv, g_send, g_recv, s_send, s_recv,
    u_send, u_recv, d_send, d_recv,
):
    chain, nd, count, blocks, chunks, heads, ratio, window = cfg
    c = lax.axis_index("ctx")
    d = lax.axis_index("dp")
    chips = nd // 2
    m, core = d // 2, lax.rem(d, 2)
    wide = heads * HEAD_SIZE
    scale = query_scalar ** (-0.5)
    features = normed_ref.shape[1]
    has_next, has_prev = c < chain - 1, c > 0

    def chip_at(mask):
        return {"dp": flipped(m, mask) * 2 + core}

    sibling = {"dp": m * 2 + 1 - core}
    after, before = {"ctx": c + 1}, {"ctx": c - 1}

    barrier = pltpu.get_barrier_semaphore()

    @pl.when(has_next)
    def _():
        pl.semaphore_signal(barrier, inc=1, device_id=after, device_id_type=MESH)

    @pl.when(has_prev)
    def _():
        pl.semaphore_signal(barrier, inc=1, device_id=before, device_id_type=MESH)

    for r in range(1, chips):
        pl.semaphore_signal(barrier, inc=1, device_id=chip_at(r), device_id_type=MESH)
    pl.semaphore_signal(barrier, inc=1, device_id=sibling, device_id_type=MESH)

    for s in range(1, blocks):
        @pl.when(c < s)
        def _():
            kbuf[s - 1] = jnp.zeros_like(kbuf[s - 1])
            vbuf[s - 1] = jnp.zeros_like(vbuf[s - 1])

    own_ids = ids_ref[:, pl.ds(pl.multiple_of(c * count, count), count)]
    query_ids = jnp.transpose(jnp.broadcast_to(own_ids, (count, count)))
    row = lax.broadcasted_iota(jnp.int32, (count, count), 0)
    col = lax.broadcasted_iota(jnp.int32, (count, count), 1)
    for s in range(blocks):
        at = jnp.maximum(c - s, 0)
        key_ids = ids_ref[:, pl.ds(pl.multiple_of(at * count, count), count)]
        offset = row - col + s * count
        good = (query_ids == key_ids) & (offset >= 0) & (offset < window) & (offset <= c * count + row)
        bias[:, s * count : (s + 1) * count] = jnp.where(good, 0.0, -jnp.inf)

    pl.semaphore_wait(barrier, has_next.astype(jnp.int32) + has_prev.astype(jnp.int32) + chips)

    def remote(src, dst, send, recv, where):
        return pltpu.make_async_remote_copy(
            src_ref=src, dst_ref=dst, send_sem=send, recv_sem=recv, device_id=where, device_id_type=MESH
        )

    def kv_copy(h, s, i):
        cols = pl.ds(pl.multiple_of(h * wide, wide), wide)
        own, buf = ((k_ref, kbuf), (v_ref, vbuf))[i]
        return remote(
            (own if s == 1 else buf.at[s - 2]).at[:, cols], buf.at[s - 1].at[:, cols],
            kv_send.at[h, s - 1, i], kv_recv.at[h, s - 1, i], after,
        )

    def kv_copies(h, s):
        return [kv_copy(h, s, i) for i in range(2)]

    def back_copy(h, s, i):
        cols = pl.ds(pl.multiple_of(h * wide, wide), wide)
        src, dst = ((dv_out, dv_in), (dk_out, dk_in))[i]
        return remote(
            src.at[s - 1].at[:, cols], dst.at[s - 1].at[:, cols],
            back_send.at[h, s - 1, i], back_recv.at[h, s - 1, i], before,
        )

    def send_own(h):
        @pl.when(has_next)
        def _():
            for copy in kv_copies(h, 1):
                copy.start()

    def forward(h):
        for s in range(1, blocks):
            @pl.when(c >= s)
            def _():
                for copy in kv_copies(h, s):
                    copy.wait_recv()

            if s + 1 < blocks:
                @pl.when((c >= s) & has_next)
                def _():
                    for copy in kv_copies(h, s + 1):
                        copy.start()

    half = (features // 256) * 128
    parts = ((0, half), (half, features - half))

    def n_copy(r, part, src, to):
        lo, size = parts[part]
        return remote(
            src.at[:, lo : lo + size], nbuf.at[r - 1].at[:, lo : lo + size],
            n_send.at[r - 1, part], n_recv.at[r - 1, part], chip_at(to),
        )

    relay = chips == 4

    def turn_part(r, part):
        src = normed_ref if r == 0 else nbuf.at[r - 1]
        lo, size = parts[part]

        def one(t, carry):
            cols = pl.ds(pl.multiple_of(lo + t * 128, 128), 128)
            turned[cols, r * count : (r + 1) * count] = jnp.transpose(src[:, cols])
            return carry

        lax.fori_loop(0, size // 128, one, 0, unroll=3)

    def n_first():
        if relay:
            for r, part in ((1, 0), (2, 1), (1, 1), (2, 0)):
                n_copy(r, part, normed_ref, r).start()
        else:
            for r in range(1, chips):
                for part in range(2):
                    n_copy(r, part, normed_ref, r).start()

    def n_relay():
        if relay:
            n_copy(1, 0, normed_ref, 1).wait_recv()
            n_copy(3, 0, nbuf.at[0], 2).start()
            n_copy(2, 1, normed_ref, 2).wait_recv()
            n_copy(3, 1, nbuf.at[1], 1).start()
            turn_part(1, 0)
            turn_part(2, 1)

    def n_finish():
        for r in range(1, chips):
            for part in range(2):
                copy = n_copy(r, part, normed_ref, r)
                if not (relay and (r, part) in ((1, 0), (2, 1))):
                    copy.wait_recv()
                copy.wait_send()
        if relay:
            for r, part in ((1, 1), (2, 0), (3, 0), (3, 1)):
                turn_part(r, part)

    def compute(h):
        for g in range(heads):
            head = h * heads + g
            kv_cols = pl.ds(pl.multiple_of(head * HEAD_SIZE, HEAD_SIZE), HEAD_SIZE)

            def stacked(ref):
                return jnp.concatenate(
                    [
                        ref[:, pl.ds(pl.multiple_of((head * ratio + z) * HEAD_SIZE, HEAD_SIZE), HEAD_SIZE)]
                        for z in range(ratio)
                    ],
                    axis=0,
                )

            q, do = stacked(q_ref), stacked(do_ref)
            keys = jnp.concatenate([k_ref[:, kv_cols]] + [kbuf[s - 1, :, kv_cols] for s in range(1, blocks)], axis=0)
            values = jnp.concatenate([v_ref[:, kv_cols]] + [vbuf[s - 1, :, kv_cols] for s in range(1, blocks)], axis=0)
            scores = mm(q, keys, 1, 1) * scale
            scores = scores + jnp.concatenate([bias[...]] * ratio, axis=0)
            top = jnp.max(scores, axis=1, keepdims=True)
            expanded = jnp.exp(scores - top)
            weights = expanded * (1.0 / jnp.sum(expanded, axis=1, keepdims=True))
            low = weights.astype(jnp.bfloat16)
            grad_probs = mm(do, values, 1, 1)
            delta = jnp.sum(low.astype(jnp.float32) * grad_probs, axis=1, keepdims=True)
            grad_scores = (weights * (grad_probs - delta)).astype(jnp.bfloat16)
            dq = (mm(grad_scores, keys, 1, 0) * scale).astype(jnp.bfloat16)
            for z in range(ratio):
                dq_ref[:, pl.ds(pl.multiple_of((head * ratio + z) * HEAD_SIZE, HEAD_SIZE), HEAD_SIZE)] = dq[
                    z * count : (z + 1) * count
                ]
            dv = mm(low, do, 0, 0)
            dk = mm(grad_scores, q, 0, 0) * scale
            for s in range(blocks):
                own_dv[s, :, kv_cols] = dv[s * count : (s + 1) * count]
                own_dk[s, :, kv_cols] = dk[s * count : (s + 1) * count]

    def give_back(h, last, which):
        cols = pl.ds(pl.multiple_of(h * wide, wide), wide)
        own, into, out, final = ((own_dv, dv_in, dv_out, dv_ref), (own_dk, dk_in, dk_out, dk_ref))[which]
        for s in range(blocks - 1, -1, -1):
            takes = not last and s + 1 < blocks

            def total():
                value = own[s, :, cols]
                if takes:
                    value = value + into[s, :, cols].astype(jnp.float32)
                return value.astype(jnp.bfloat16)

            if s > 0:
                @pl.when(c >= s)
                def _():
                    if takes:
                        back_copy(h, s + 1, which).wait_recv()
                    out[s - 1, :, cols] = total()
                    back_copy(h, s, which).start()
            else:
                if takes:
                    back_copy(h, 1, which).wait_recv()
                final[:, cols] = total()

    lag = jnp.where(c == chain - 1, 0, jnp.where(c == chain - 2, min(3, chunks), chunks))
    end = chunks - 1
    relay_at = jnp.where(c == chain - 1, chunks // 2, end)
    held = min(2, chunks)
    send_own(0)
    if chunks > 1:
        send_own(1)
    n_first()
    if relay:
        turn_part(0, 0)
        turn_part(0, 1)

    def chunk(i, carry):
        @pl.when(i < chunks)
        def _():
            forward(i)

            @pl.when(i + 2 < chunks)
            def _():
                send_own(i + 2)

            compute(i)

        j = i - lag
        turn = (j >= 0) & (j < end)

        @pl.when(turn & (c == chain - 1))
        def _():
            give_back(j, True, 0)

            @pl.when(j < chunks - held)
            def _():
                give_back(j, True, 1)

        @pl.when(turn & has_next)
        def _():
            give_back(j, False, 0)

            @pl.when(j < chunks - held)
            def _():
                give_back(j, False, 1)

        @pl.when(i == relay_at)
        def _():
            n_relay()

        return carry

    lax.fori_loop(0, 2 * chunks, chunk, 0)

    @pl.when(c == chain - 1)
    def _():
        give_back(end, True, 0)

    @pl.when(has_next)
    def _():
        give_back(end, False, 0)

    pair = gbuf.shape[2]
    cw = pair // 2

    def g_copy(r):
        to = flipped(m, r)
        return remote(
            dv_ref.at[:, pl.ds(pl.multiple_of(to * pair, pair), pair)], gbuf.at[r - 1],
            g_send.at[r - 1], g_recv.at[r - 1], chip_at(r),
        )

    for r in range(1, chips):
        g_copy(r).start()

    for e in range(chunks - held, chunks):
        @pl.when(c == chain - 1)
        def _():
            give_back(e, True, 1)

        @pl.when(has_next)
        def _():
            give_back(e, False, 1)

    n_finish()
    for r in range(1, chips):
        g_copy(r).wait_recv()

    own_g = dv_ref[:, pl.ds(pl.multiple_of(m * pair, pair), pair)]
    tile = 384 if features % 384 == 0 else 128

    def w_tile(t, carry):
        cols = pl.ds(pl.multiple_of(t * tile, tile), tile)
        acc = mm(normed_ref[:, cols], own_g, 0, 0)
        for r in range(1, chips):
            acc = acc + mm(nbuf[r - 1, :, cols], gbuf[r - 1], 0, 0)
        w_store(cols, acc)
        return carry

    def w_store(cols, acc):
        low = acc[:, :cw]
        high = acc[:, cw:] if cw % 128 == 0 else pltpu.roll(acc, cw, 1)[:, :cw]
        first = core == 0
        w_own[cols, :] = jnp.where(first, low, high)
        w_send[cols, :] = jnp.where(first, high, low).astype(jnp.bfloat16)

    if not relay:
        lax.fori_loop(0, features // tile, w_tile, 0)
    all_g = jnp.concatenate([own_g] + [gbuf[r - 1] for r in range(1, chips)], axis=0)

    rows = features // chain
    subs = r_send.shape[0] // chain
    step = rows // subs
    whole = chain * subs

    def s_copy(p):
        span = pl.ds(pl.multiple_of(p * step, 16), step)
        return remote(w_send.at[span], w_sib.at[span], s_send.at[p], s_recv.at[p], sibling)

    def u_copy(p):
        return remote(r_send.at[p], r_up.at[p], u_send.at[p], u_recv.at[p], after)

    def d_copy(p):
        return remote(r_send.at[p], r_down.at[p], d_send.at[p], d_recv.at[p], before)

    def up_index(u):
        return (chain - 1 - u // subs) * subs + lax.rem(u, subs)

    def send_sib(t, carry):
        flip = jnp.where(c < chain - c, up_index(t), t)
        if relay:
            span = pl.ds(pl.multiple_of(flip * step, 16), step)
            w_store(span, mm(turned[span, :], all_g, 1, 0))
        s_copy(flip).start()
        return carry

    lax.fori_loop(0, whole, send_sib, 0)

    def sums(p, extra):
        base = pl.ds(pl.multiple_of(p * step, 16), step)
        value = w_own[base, :] + w_sib[base, :].astype(jnp.float32)
        for ref in extra:
            value = value + ref[p].astype(jnp.float32)
        return value

    def reduce_step(tau, carry):
        u = tau - 2 * c
        v = tau - 2 * (chain - 1 - c)

        @pl.when((u >= 0) & (u < (chain - 1 - c) * subs))
        def _():
            p = up_index(u)
            s_copy(p).wait_recv()

            @pl.when(c == 0)
            def _():
                r_send[p] = sums(p, ()).astype(jnp.bfloat16)

            @pl.when(c > 0)
            def _():
                u_copy(p).wait_recv()
                r_send[p] = sums(p, (r_up,)).astype(jnp.bfloat16)

            u_copy(p).start()

        @pl.when((v >= 0) & (v < c * subs))
        def _():
            s_copy(v).wait_recv()

            @pl.when(c == chain - 1)
            def _():
                r_send[v] = sums(v, ()).astype(jnp.bfloat16)

            @pl.when(c < chain - 1)
            def _():
                d_copy(v).wait_recv()
                r_send[v] = sums(v, (r_down,)).astype(jnp.bfloat16)

            d_copy(v).start()

        return carry

    lax.fori_loop(0, (chain - 1) * (subs + 2), reduce_step, 0)

    final_scale = (count * chain * nd) ** (-0.5)

    def finish(t, carry):
        p = c * subs + t
        s_copy(p).wait_recv()
        span = pl.ds(pl.multiple_of(t * step, 16), step)

        @pl.when(has_prev)
        def _():
            u_copy(p).wait_recv()

        @pl.when(has_next)
        def _():
            d_copy(p).wait_recv()

        @pl.when(c == 0)
        def _():
            dw_ref[span, :] = (sums(p, (r_down,)) * final_scale).astype(jnp.bfloat16)

        @pl.when(c == chain - 1)
        def _():
            dw_ref[span, :] = (sums(p, (r_up,)) * final_scale).astype(jnp.bfloat16)

        @pl.when(has_prev & has_next)
        def _():
            dw_ref[span, :] = (sums(p, (r_up, r_down)) * final_scale).astype(jnp.bfloat16)

        return carry

    lax.fori_loop(0, subs, finish, 0)

    def drain(h, carry):
        for s in range(1, blocks):
            @pl.when(has_next & (c >= s - 1))
            def _():
                for copy in kv_copies(h, s):
                    copy.wait_send()

            @pl.when(c >= s)
            def _():
                for i in range(2):
                    back_copy(h, s, i).wait_send()
        return carry

    lax.fori_loop(0, chunks, drain, 0)
    for r in range(1, chips):
        g_copy(r).wait_send()

    def drain_pieces(p, carry):
        s_copy(p).wait_send()

        @pl.when(p >= (c + 1) * subs)
        def _():
            u_copy(p).wait_send()

        @pl.when(p < c * subs)
        def _():
            d_copy(p).wait_send()

        return carry

    lax.fori_loop(0, whole, drain_pieces, 0)


def body(normed, queries, keys, values, out_grad, segment_ids):
    count = queries.shape[1]
    width = keys.shape[2]
    features = normed.shape[2]
    chain, nd = lax.axis_size("ctx"), lax.axis_size("dp")
    chips = nd // 2
    blocks = min(-(-WINDOW // count), chain - 1) + 1
    groups = width // HEAD_SIZE
    heads = max(1, groups // 8)
    chunks = groups // heads
    ratio = queries.shape[2] // width
    cw = width // nd
    rows = features // chain
    subs = max(n for n in range(1, 5) if rows % (16 * n) == 0)
    pieces = chain * subs
    bf, f32 = jnp.bfloat16, jnp.float32
    vm = pltpu.VMEM
    dma = pltpu.SemaphoreType.DMA
    back = blocks - 1
    cfg = (chain, nd, count, blocks, chunks, heads, ratio, WINDOW)
    out = pl.pallas_call(
        functools.partial(kernel, cfg),
        out_shape=(
            jax.ShapeDtypeStruct(queries.shape[1:], bf),
            jax.ShapeDtypeStruct(keys.shape[1:], bf),
            jax.ShapeDtypeStruct(keys.shape[1:], bf),
            jax.ShapeDtypeStruct((rows, cw), bf),
        ),
        in_specs=[pl.BlockSpec(memory_space=vm)] * 6,
        out_specs=(pl.BlockSpec(memory_space=vm),) * 4,
        scratch_shapes=[
            vm((back, count, width), bf), vm((back, count, width), bf),
            vm((back, count, width), bf), vm((back, count, width), bf),
            vm((back, count, width), bf), vm((back, count, width), bf),
            vm((blocks, count, width), f32), vm((blocks, count, width), f32),
            vm((count, blocks * count), f32),
            vm((chips - 1, count, features), bf), vm((chips - 1, count, 2 * cw), bf),
            vm((features, chips * count) if chips == 4 else (16, 128), bf),
            vm((features, cw), f32), vm((features, cw), bf), vm((features, cw), bf),
            vm((pieces, rows // subs, cw), bf), vm((pieces, rows // subs, cw), bf), vm((pieces, rows // subs, cw), bf),
            dma((chunks, back, 2)), dma((chunks, back, 2)), dma((chunks, back, 2)), dma((chunks, back, 2)),
            dma((chips - 1, 2)), dma((chips - 1, 2)), dma((chips - 1,)), dma((chips - 1,)),
            dma((pieces,)), dma((pieces,)), dma((pieces,)), dma((pieces,)), dma((pieces,)), dma((pieces,)),
        ],
        compiler_params=pltpu.CompilerParams(
            collective_id=0, has_side_effects=True, vmem_limit_bytes=64000 * 1024
        ),
    )(normed[0], queries[0], keys[0], values[0], out_grad[0], segment_ids)
    return out[0][None], out[1][None], out[2][None], out[3]


def solution(mesh):
    placed = (P("dp", "ctx", None),) * 5 + (P("dp", None),)
    return jax.shard_map(
        body,
        mesh=mesh,
        in_specs=placed,
        out_specs=(
            P("dp", "ctx", None),
            P("dp", "ctx", None),
            P("dp", "ctx", None),
            P("ctx", "dp"),
        ),
        check_vma=False,
    )
```
